32 devices in a mesh: groups: 2 (over y), req: 2 (over core), ctx: 8 (over z, x).
Axes of the slice: x: 2, y: 2, z: 4, core: 2. Of those that a mesh axis runs over, the one named last changes fastest.
Arguments:
- queries: bfloat16 [4, 1024, 4096], P(('groups', 'req'), 'ctx'), parts along dimension 0, may hold values from -6 to 6
- keys: bfloat16 [4, 1024, 512], P(('groups', 'req'), 'ctx'), parts along dimension 0, may hold values from -6 to 6
- values: bfloat16 [4, 1024, 512], P(('groups', 'req'), 'ctx'), parts along dimension 0, may hold values from -6 to 6
- cache_keys: bfloat16 [16, 256, 512], P(('groups', 'ctx')), parts along dimension 0, may hold values from -6 to 6
- cache_values: bfloat16 [16, 256, 512], P(('groups', 'ctx')), parts along dimension 0, may hold values from -6 to 6
- doc_lengths: int32 [4], P('groups'), parts along dimension 0, may hold values from 32 to 256, as said below
- doc_owners: int32 [4], P('groups'), parts along dimension 0, may hold values from 0 to 7, as said below
- block_offsets: int32 [4], P('groups'), parts along dimension 0, may hold values from 1 to 7
Outputs:
- attended: bfloat16 [4, 1024, 4096], P(('groups', 'req'), 'ctx'), parts along dimension 0
The draws below stay inside these ranges and needn't reach their ends.
There are 2 independent parts, one for each index of `groups`. The reference program is written for one: setup_inputs(seed, part) draws one part's arguments, and reference() takes and returns one part's arrays. A program takes and returns all parts, laid end to end along the dimension named above; each array names one. Nothing has to cross between parts.
Inputs may be any that keep to these rules, and one draw needn't show every extreme that they name: `doc_lengths`: one document block has exactly 256 live rows. `doc_owners`: the owners of the two document blocks differ.
All inputs are finite; a program needn't handle non-finite values.
Results may differ from the reference program's by a relative error of at most 0.0065.
Values may be sent and summed in bfloat16 or wider, within the bound.
No kernel may reach another device: no remote copies, remote signals or barrier semaphores. Data moves between devices by JAX's collectives and lax.ppermute only.
A program may use at most 64 MiB of HBM per device.

```python
import math
import jax
import jax.numpy as jnp
from jax import lax

HD = 128
QH = 32
KVH = 4
TOK_DEV = 128
HOPS = 3
DOCS = 2
DOCLEN = 256
REQS = 2
BLOCKS = 8
SEQ = 1024


def draw_queries(key, part):
    drawn = jnp.clip(jax.random.normal(jax.random.fold_in(key, 11), (REQS, SEQ, QH * HD), jnp.float32), -6.0, 6.0)
    return drawn.astype(jnp.bfloat16)


def draw_keys(key, part):
    drawn = jnp.clip(jax.random.normal(jax.random.fold_in(key, 12), (REQS, SEQ, KVH * HD), jnp.float32), -6.0, 6.0)
    return drawn.astype(jnp.bfloat16)


def draw_doc_lengths(key, part):
    chosen = jax.random.randint(jax.random.fold_in(key, 21), (), 0, DOCS)
    others = jax.random.randint(jax.random.fold_in(key, 22), (DOCS,), DOCLEN // 8, DOCLEN + 1)
    return jnp.where(jnp.arange(DOCS) == chosen, DOCLEN, others).astype(jnp.int32)


def draw_doc_owners(key, part):
    first = jax.random.randint(jax.random.fold_in(key, 41), (), 0, BLOCKS)
    stride = jax.random.randint(jax.random.fold_in(key, 42), (), 1, BLOCKS)
    return jnp.stack([first, (first + stride) % BLOCKS]).astype(jnp.int32)


def levels(stream_key, shape, split, smallest, top_value):
    gain, own = 1.0, jax.random.fold_in(stream_key, 6)
    for dim, shards_of in split:
        heights = jnp.exp(jax.random.uniform(jax.random.fold_in(own, dim), (shards_of,), jnp.float32, smallest / len(split), top_value / len(split)))
        gain = gain * jnp.repeat(heights, shape[dim] // shards_of).reshape([-1 if axis == dim else 1 for axis in range(len(shape))])
    return gain


def bell_draw(own_key, shape, scale, most, pieces=(), kind=jnp.bfloat16):
    values = jax.random.normal(own_key, shape, jnp.float32) * scale
    if len(pieces) > 0:
        values = levels(own_key, shape, pieces, -0.22, 0.18) * values
    return jnp.clip(values, min=-most, max=most).astype(kind)


def setup_inputs(seed: int = 0, part: int = 0) -> dict:
    arg_keys = jax.random.split(jax.random.key(seed), 9)
    part_splits = jax.random.split(jax.random.fold_in(arg_keys[8], part), 9)
    return {
        "queries": draw_queries(jax.random.fold_in(jax.random.fold_in(arg_keys[8], part), 71), part),
        "keys": draw_keys(jax.random.fold_in(jax.random.fold_in(arg_keys[8], part), 71), part),
        "values": bell_draw(part_splits[2], (REQS, SEQ, KVH * HD), 1.0, 6.0, ((0, 2), (1, 8))),
        "cache_keys": bell_draw(part_splits[3], (BLOCKS, DOCLEN, KVH * HD), 1.0, 6.0, ((0, 8),)),
        "cache_values": bell_draw(part_splits[4], (BLOCKS, DOCLEN, KVH * HD), 1.0, 6.0, ((0, 8),)),
        "doc_lengths": draw_doc_lengths(jax.random.fold_in(jax.random.fold_in(arg_keys[8], part), 71), part),
        "doc_owners": draw_doc_owners(jax.random.fold_in(jax.random.fold_in(arg_keys[8], part), 71), part),
        "block_offsets": jax.random.randint(part_splits[7], (REQS,), 1, BLOCKS).astype(jnp.int32),
    }


NEGATIVE = -1e+30

def attend_rows(query_block, key_rows, value_rows, allowed):
    tokens = query_block.shape[0]
    groups = QH // KVH
    query_heads = query_block.astype(jnp.float32).reshape(tokens, KVH, groups, HD)
    key_heads = key_rows.astype(jnp.float32).reshape(key_rows.shape[0], KVH, HD)
    value_heads = value_rows.astype(jnp.float32).reshape(value_rows.shape[0], KVH, HD)
    scores = jnp.einsum('tgid,sgd->gits', query_heads, key_heads) / math.sqrt(HD)
    scores = jnp.where(allowed[None, None], scores, NEGATIVE)
    highest = lax.optimization_barrier(jnp.max(scores, axis=-1, keepdims=True))
    weights = jnp.where(allowed[None, None], jnp.exp(scores - highest), 0.0)
    denominators = lax.optimization_barrier(jnp.sum(weights, axis=-1))
    rounded = lax.optimization_barrier(weights.astype(jnp.bfloat16)).astype(jnp.float32)
    summed = jnp.einsum('gits,sgd->gitd', rounded, value_heads)
    result = summed / denominators[..., None]
    return jnp.transpose(result, (2, 0, 1, 3)).reshape(tokens, QH * HD).astype(jnp.bfloat16)

def reference(queries, keys, values, cache_keys, cache_values, doc_lengths, doc_owners, block_offsets):
    kv_width = KVH * HD
    doc_keys = jnp.take(cache_keys, doc_owners, axis=0).reshape(DOCS * DOCLEN, kv_width)
    doc_values = jnp.take(cache_values, doc_owners, axis=0).reshape(DOCS * DOCLEN, kv_width)
    doc_live = (jnp.arange(DOCLEN)[None, :] < doc_lengths[:, None]).reshape(DOCS * DOCLEN)
    inside = jnp.arange(TOK_DEV)
    causal = inside[None, :] <= inside[:, None]
    query_blocks = queries.reshape(REQS * BLOCKS, TOK_DEV, QH * HD)
    key_blocks = keys.reshape(REQS * BLOCKS, TOK_DEV, kv_width)
    value_blocks = values.reshape(REQS * BLOCKS, TOK_DEV, kv_width)

    def one_block(flat_index):
        request = flat_index // BLOCKS
        slot_index = flat_index % BLOCKS
        offset = lax.dynamic_index_in_dim(block_offsets, request, 0, keepdims=False)
        placed = (slot_index - offset) % BLOCKS
        key_list = []
        value_list = []
        allowed_list = []
        for hop_count in range(HOPS + 1):
            source = (request * BLOCKS + (slot_index - hop_count) % BLOCKS).astype(jnp.int32)
            key_list.append(lax.dynamic_index_in_dim(key_blocks, source, 0, keepdims=False))
            value_list.append(lax.dynamic_index_in_dim(value_blocks, source, 0, keepdims=False))
            if hop_count == 0:
                allowed_list.append(causal)
            else:
                allowed_list.append(jnp.broadcast_to(placed - hop_count >= 0, (TOK_DEV, TOK_DEV)))
        key_list.append(doc_keys)
        value_list.append(doc_values)
        allowed_list.append(jnp.broadcast_to(doc_live[None, :], (TOK_DEV, DOCS * DOCLEN)))
        query_block = lax.dynamic_index_in_dim(query_blocks, flat_index, 0, keepdims=False)
        return attend_rows(query_block, jnp.concatenate(key_list, axis=0), jnp.concatenate(value_list, axis=0), jnp.concatenate(allowed_list, axis=1))
    attended = lax.map(one_block, jnp.arange(REQS * BLOCKS, dtype=jnp.int32))
    return attended.reshape(REQS, BLOCKS * TOK_DEV, QH * HD)
```

```python
import functools
import math

import jax
import jax.numpy as jnp
from jax import lax
from jax.experimental import pallas as pl
from jax.experimental.pallas import tpu as pltpu
from jax.sharding import PartitionSpec as P

HD = 128
HOPS = 3
DOCS = 2
RING_LIMIT = 16

NEGATIVE = -1e30
SCALE = math.log2(math.e) / math.sqrt(HD)


def broadcast(block, axis, source):
    block = jnp.where(lax.axis_index(axis) == source, block, jnp.zeros_like(block))
    return lax.psum(block, axis)


def shifted(value, axis, steps):
    count = lax.axis_size(axis)
    pairs = [(source, (source + steps) % count) for source in range(count)]
    return lax.ppermute(value, axis, pairs)


def attention_body(rows, group, tile, own, *refs):
    count = len(rows)
    live, q_ref = refs[0], refs[1]
    key_refs, value_refs = refs[2 : 2 + count], refs[2 + count : 2 + 2 * count]
    out_ref, keys, values = refs[2 + 2 * count :]
    total = sum(rows)
    starts = [sum(rows[:number]) for number in range(count)]
    tokens = q_ref.shape[0]

    @pl.when(pl.program_id(0) == 0)
    def _():
        values[:, HD:] = jnp.ones((total, HD), jnp.bfloat16)
        for number, (start, height) in enumerate(zip(starts, rows)):
            lane = lax.broadcasted_iota(jnp.int32, (height, HD), 1)
            row = lax.broadcasted_iota(jnp.int32, (height, HD), 0)
            dead = (row >= live[number]) & (lane == 0)
            keys[start : start + height, HD:] = jnp.where(dead, NEGATIVE, 0.0).astype(jnp.bfloat16)

    for key_ref, value_ref, start, height in zip(key_refs, value_refs, starts, rows):
        keys[start : start + height, :HD] = key_ref[...].reshape(height, HD)
        values[start : start + height, :HD] = value_ref[...].reshape(height, HD)

    lane = lax.broadcasted_iota(jnp.int32, (tile * tokens, HD), 1)
    first = jnp.where(lane == 0, 1.0, 0.0).astype(jnp.bfloat16)
    query = lax.broadcasted_iota(jnp.int32, (tokens, rows[own]), 0)
    key = lax.broadcasted_iota(jnp.int32, (tokens, rows[own]), 1)
    causal = jnp.concatenate([key <= query] * tile, axis=0)
    for head in range(0, group, tile):
        heads = [q_ref[:, (head + i) * HD : (head + i + 1) * HD] for i in range(tile)]
        block = jnp.concatenate([jnp.concatenate(heads, axis=0), first], axis=1)
        scores = lax.dot_general(
            block, keys[...], (((1,), (1,)), ((), ())), preferred_element_type=jnp.float32
        )
        begin, end = starts[own], starts[own] + rows[own]
        masked = jnp.where(causal, scores[:, begin:end], NEGATIVE)
        pieces = [scores[:, :begin], masked, scores[:, end:]]
        scores = jnp.concatenate([piece for piece in pieces if piece.shape[1]], axis=1)
        highest = jnp.max(scores, axis=1, keepdims=True) * SCALE
        weights = jnp.exp2(scores * SCALE - highest).astype(jnp.bfloat16)
        summed = jnp.dot(weights, values[...], preferred_element_type=jnp.float32)
        result = (summed[:, :HD] / summed[:, HD:]).astype(jnp.bfloat16)
        for i in range(tile):
            out_ref[:, (head + i) * HD : (head + i + 1) * HD] = result[i * tokens : (i + 1) * tokens]


def attention(live, queries, segments, own):
    tokens, width = queries.shape
    kv_heads = segments[0][0].shape[-1] // HD
    group = width // HD // kv_heads
    rows = tuple(segment[4] for segment in segments)

    def spec(array, lead, height):
        return pl.BlockSpec((1,) * len(lead) + (height, HD), lambda g, s: (*lead, 0, g))

    heads = pl.BlockSpec((tokens, group * HD), lambda g, s: (0, g))
    return pl.pallas_call(
        functools.partial(attention_body, rows, group, 2 if group % 2 == 0 else 1, own),
        out_shape=jax.ShapeDtypeStruct((tokens, width), jnp.bfloat16),
        grid_spec=pltpu.PrefetchScalarGridSpec(
            num_scalar_prefetch=1,
            grid=(kv_heads,),
            in_specs=[heads]
            + [spec(segment[0], segment[1], segment[4]) for segment in segments]
            + [spec(segment[2], segment[3], segment[4]) for segment in segments],
            out_specs=heads,
            scratch_shapes=[pltpu.VMEM((sum(rows), 2 * HD), jnp.bfloat16)] * 2,
        ),
        compiler_params=pltpu.CompilerParams(vmem_limit_bytes=48 << 20),
    )(live, queries, *[s[0] for s in segments], *[s[2] for s in segments])


def pick_body(holds, picks, *refs):
    pieces, out_ref, sems = refs[: len(holds)], refs[len(holds)], refs[len(holds) + 1]
    for act in ("start", "wait"):
        for number in range(DOCS):
            for (delta, begin), piece in zip(holds, pieces):

                @pl.when(picks[number] == delta)
                def _():
                    target = out_ref.at[number, :, pl.ds(begin, piece.shape[1])]
                    slot = sems.at[number, 0 if begin == 0 else 1]
                    copy = pltpu.make_async_copy(piece, target, slot)
                    getattr(copy, act)()


def pick(picks, holds, pieces, shape):
    return pl.pallas_call(
        functools.partial(pick_body, holds),
        out_shape=jax.ShapeDtypeStruct((DOCS,) + shape, jnp.bfloat16),
        grid_spec=pltpu.PrefetchScalarGridSpec(
            num_scalar_prefetch=1,
            grid=(1,),
            in_specs=[pl.BlockSpec(memory_space=pl.ANY)] * len(pieces),
            out_specs=pl.BlockSpec((DOCS,) + shape, lambda i, s: (0, 0, 0, 0)),
            scratch_shapes=[pltpu.SemaphoreType.DMA((DOCS, 2))],
        ),
    )(picks, *pieces)


def ring_documents(cache_keys, cache_values, doc_owners):
    count = lax.axis_size("ctx")
    cores = lax.axis_size("req")
    core = lax.axis_index("req")
    ring = list(range(0, count, 2)) + list(range(1, count, 2))[::-1]
    place = jnp.array([ring.index(index) for index in range(count)], jnp.int32)
    doc_rows = cache_keys.shape[1]
    half = doc_rows // cores
    mine = [lax.dynamic_slice_in_dim(part[0], core * half, half, 0) for part in (cache_keys, cache_values)]
    mine = jnp.stack(mine)
    onward = [(ring[i], ring[(i + 1) % count]) for i in range(count)]
    backward = [(target, source) for source, target in onward]
    holds, pieces = [(0, 0)], [mine]
    ahead = behind = mine
    for step in range(1, count // 2 + 1):
        if 2 * step < count:
            ahead = lax.ppermute(ahead, "ctx", onward)
            behind = lax.ppermute(behind, "ctx", backward)
            holds += [(count - step, 0), (step, 0)]
            pieces += [ahead, behind]
        else:
            cut = half // 2
            upper = lax.ppermute(ahead[:, :cut], "ctx", onward)
            lower = lax.ppermute(behind[:, cut:], "ctx", backward)
            holds += [(step, 0), (step, cut)]
            pieces += [upper, lower]
    picks = (place[doc_owners] - place[lax.axis_index("ctx")]) % count
    held = pick(picks, holds, pieces, mine.shape)
    other = shifted(held, "req", 1)
    return [(held, core * half), (other, (1 - core) * half)]


def summed_documents(cache_keys, cache_values, doc_owners):
    cached = jnp.stack([cache_keys[0], cache_values[0]])
    docs = jnp.stack([broadcast(cached, "ctx", doc_owners[number]) for number in range(DOCS)])
    return [(docs, 0)]


def per_device(
    queries, keys, values, cache_keys, cache_values, doc_lengths, doc_owners, block_offsets
):
    count = lax.axis_size("ctx")
    position = lax.axis_index("ctx")
    request = lax.axis_index("req")
    tokens = queries.shape[1]
    offset = jnp.sum(jnp.where(jnp.arange(block_offsets.shape[0]) == request, block_offsets, 0))
    placed = (position - offset) % count
    even = position % 2 == 0

    own = jnp.stack([keys[0], values[0]])
    two = shifted(own, "ctx", 2)
    swapped = lax.ppermute(two, "ctx", [(i, i ^ 1) for i in range(count)])
    passed = shifted(jnp.where(even, own, two), "ctx", 1)
    hop_of_swapped = jnp.where(even, 1, HOPS)
    hop_of_passed = jnp.where(even, HOPS, 1)

    if lax.axis_size("req") == 2 and count <= RING_LIMIT:
        documents = ring_documents(cache_keys, cache_values, doc_owners)
    else:
        documents = summed_documents(cache_keys, cache_values, doc_owners)

    blocks = [(own, tokens), (two, jnp.where(placed >= 2, tokens, 0))]
    blocks += [(swapped, jnp.where(placed >= hop_of_swapped, tokens, 0))]
    blocks += [(passed, jnp.where(placed >= hop_of_passed, tokens, 0))]
    live = [jnp.asarray(count_of, jnp.int32) for _, count_of in blocks]
    segments = [(block, (0,), block, (1,), tokens) for block, _ in blocks]
    for docs, begin in documents:
        for number in range(DOCS):
            segments.append((docs, (number, 0), docs, (number, 1), docs.shape[2]))
            live.append(doc_lengths[number] - begin)
    return attention(jnp.stack(live), queries[0], segments, 0)[None]


def solution(mesh):
    return jax.shard_map(
        per_device,
        mesh=mesh,
        in_specs=(
            P(("groups", "req"), "ctx", None),
            P(("groups", "req"), "ctx", None),
            P(("groups", "req"), "ctx", None),
            P(("groups", "ctx"), None, None),
            P(("groups", "ctx"), None, None),
            P("groups"),
            P("groups"),
            P("groups"),
        ),
        out_specs=P(("groups", "req"), "ctx", None),
        check_vma=False,
    )
```

```python
import functools
import math

import jax
import jax.numpy as jnp
from jax import lax
from jax.experimental import pallas as pl
from jax.experimental.pallas import tpu as pltpu
from jax.sharding import PartitionSpec as P

HD = 128
HOPS = 3
DOCS = 2
RING_LIMIT = 16

NEGATIVE = -1e30
SCALE = math.log2(math.e) / math.sqrt(HD)


def broadcast(block, axis, source):
    block = jnp.where(lax.axis_index(axis) == source, block, jnp.zeros_like(block))
    return lax.psum(block, axis)


def shifted(value, axis, steps):
    count = lax.axis_size(axis)
    pairs = [(source, (source + steps) % count) for source in range(count)]
    return lax.ppermute(value, axis, pairs)

def score_tile(block, keys, values, carried, causal, begin, end):
    scores = lax.dot_general(
        block, keys[...], (((1,), (1,)), ((), ())), preferred_element_type=jnp.float32
    )
    if causal is not None:
        masked = jnp.where(causal, scores[:, begin:end], NEGATIVE)
        pieces = [scores[:, :begin], masked, scores[:, end:]]
        scores = jnp.concatenate([piece for piece in pieces if piece.shape[1]], axis=1)
    highest = jnp.max(scores, axis=1, keepdims=True) * SCALE
    if carried is not None:
        highest = jnp.maximum(highest, carried[:, :1])
    weights = jnp.exp2(scores * SCALE - highest).astype(jnp.bfloat16)
    return jnp.dot(weights, values[...], preferred_element_type=jnp.float32), highest


def bias_rows(keys, start, height, live):
    lane = lax.broadcasted_iota(jnp.int32, (height, HD), 1)
    row = lax.broadcasted_iota(jnp.int32, (height, HD), 0)
    dead = (row >= live) & (lane == 0)
    keys[start : start + height, HD:] = jnp.where(dead, NEGATIVE, 0.0).astype(jnp.bfloat16)


def query_tile(q_ref, head, tile):
    heads = [q_ref[:, (head + i) * HD : (head + i + 1) * HD] for i in range(tile)]
    rows = jnp.concatenate(heads, axis=0)
    lane = lax.broadcasted_iota(jnp.int32, rows.shape, 1)
    return jnp.concatenate([rows, jnp.where(lane == 0, 1.0, 0.0).astype(jnp.bfloat16)], axis=1)


def ring_place(index, count):
    return jnp.where(index % 2 == 0, index // 2, count - 1 - index // 2)


def window_body(group, tile, offsets, q_ref, own, two, swapped, passed, out_ref, log_ref, keys, values):
    count = lax.axis_size("ctx")
    tokens = q_ref.shape[0]
    position = lax.axis_index("ctx")
    placed = lax.rem(position - offsets[lax.axis_index("req")] + count, count)
    even = lax.rem(position, 2) == 0
    hops = (0, 2, jnp.where(even, 1, HOPS), jnp.where(even, HOPS, 1))

    @pl.when(pl.program_id(0) == 0)
    def _():
        values[:, HD:] = jnp.ones((values.shape[0], HD), jnp.bfloat16)
        for number, hop in enumerate(hops):
            bias_rows(keys, number * tokens, tokens, jnp.where(placed >= hop, tokens, 0))

    for number, ref in enumerate((own, two, swapped, passed)):
        keys[number * tokens : (number + 1) * tokens, :HD] = ref[0]
        values[number * tokens : (number + 1) * tokens, :HD] = ref[1]

    query = lax.broadcasted_iota(jnp.int32, (tokens, tokens), 0)
    key = lax.broadcasted_iota(jnp.int32, (tokens, tokens), 1)
    causal = jnp.concatenate([key <= query] * tile, axis=0)
    for head in range(0, group, tile):
        block = query_tile(q_ref, head, tile)
        summed, highest = score_tile(block, keys, values, None, causal, 0, tokens)
        rows = slice(head * tokens, (head + tile) * tokens)
        out_ref[0, rows] = summed[:, :HD] / summed[:, HD:]
        log_ref[0, rows] = highest + jnp.log2(summed[:, HD:])


def document_body(
    group, tile, count, ring, owners, lengths, q_ref, in_ref, log_ref, *refs
):
    pieces = refs[:count]
    out_ref, keys, values = refs[count:]
    tokens = q_ref.shape[0]
    height = keys.shape[0] // DOCS
    head_index = pl.program_id(0)

    @pl.when(head_index == 0)
    def _():
        values[:, HD:] = jnp.ones((values.shape[0], HD), jnp.bfloat16)
        for number in range(DOCS):
            bias_rows(keys, number * height, height, lengths[number])

    columns = pl.ds(pl.multiple_of(head_index * HD, HD), HD)
    for number in range(DOCS):
        if ring:
            slots = lax.axis_size("ctx")
            gap = ring_place(lax.axis_index("ctx"), slots) - ring_place(owners[number], slots)
            gap = jnp.where(lax.axis_index("req") == 0, gap, -gap)
            gap = jnp.where(gap < 0, gap + slots, gap)
        rows = slice(number * height, (number + 1) * height)
        for index, piece in enumerate(pieces):

            @pl.when((gap if ring else number) == index)
            def _():
                keys[rows, :HD] = piece[0, :, columns]
                values[rows, :HD] = piece[1, :, columns]

    for head in range(0, group, tile):
        block = query_tile(q_ref, head, tile)
        rows = slice(head * tokens, (head + tile) * tokens)
        log = log_ref[0, rows]
        summed, highest = score_tile(block, keys, values, log, None, 0, 0)
        share = jnp.exp2(log - highest)
        total = summed[:, :HD] + in_ref[0, rows] * share
        result = (total / (summed[:, HD:] + share)).astype(jnp.bfloat16)
        for i in range(tile):
            out_ref[:, (head + i) * HD : (head + i + 1) * HD] = result[i * tokens : (i + 1) * tokens]


def attend_window(queries, blocks, block_offsets):
    tokens, width = queries.shape
    kv_heads = blocks[0].shape[-1] // HD
    group = width // HD // kv_heads
    rows = group * tokens
    partial = pl.BlockSpec((1, rows, HD), lambda g, *s: (g, 0, 0))
    total = len(blocks) * tokens
    return pl.pallas_call(
        functools.partial(window_body, group, 2 if group % 2 == 0 else 1),
        out_shape=[jax.ShapeDtypeStruct((kv_heads, rows, HD), jnp.float32)] * 2,
        grid_spec=pltpu.PrefetchScalarGridSpec(
            num_scalar_prefetch=1,
            grid=(kv_heads,),
            in_specs=[pl.BlockSpec((tokens, group * HD), lambda g, *s: (0, g))]
            + [pl.BlockSpec((2, tokens, HD), lambda g, *s: (0, 0, g))] * len(blocks),
            out_specs=[partial] * 2,
            scratch_shapes=[pltpu.VMEM((total, 2 * HD), jnp.bfloat16)] * 2,
        ),
        compiler_params=pltpu.CompilerParams(vmem_limit_bytes=32 << 20),
        cost_estimate=pl.CostEstimate(
            flops=4 * kv_heads * rows * total * HD,
            bytes_accessed=8 * kv_heads * rows * HD,
            transcendentals=kv_heads * rows * total,
        ),
        name="window",
    )(block_offsets, queries, *blocks)


def attend_documents(queries, partials, pieces, ring, doc_owners, doc_lengths):
    tokens, width = queries.shape
    doc_rows, kv_width = pieces[0].shape[1:]
    kv_heads = kv_width // HD
    group = width // HD // kv_heads
    rows = group * tokens
    heads = pl.BlockSpec((tokens, group * HD), lambda g, *s: (0, g))
    partial = pl.BlockSpec((1, rows, HD), lambda g, *s: (g, 0, 0))
    total = DOCS * doc_rows
    return pl.pallas_call(
        functools.partial(document_body, group, 2 if group % 2 == 0 else 1, len(pieces), ring),
        out_shape=jax.ShapeDtypeStruct((tokens, width), jnp.bfloat16),
        grid_spec=pltpu.PrefetchScalarGridSpec(
            num_scalar_prefetch=2,
            grid=(kv_heads,),
            in_specs=[heads, partial, partial]
            + [pl.BlockSpec(memory_space=pltpu.VMEM)] * len(pieces),
            out_specs=heads,
            scratch_shapes=[pltpu.VMEM((total, 2 * HD), jnp.bfloat16)] * 2,
        ),
        compiler_params=pltpu.CompilerParams(vmem_limit_bytes=32 << 20),
        cost_estimate=pl.CostEstimate(
            flops=4 * kv_heads * rows * total * HD,
            bytes_accessed=8 * kv_heads * rows * HD,
            transcendentals=kv_heads * rows * total,
        ),
        name="documents",
    )(doc_owners, doc_lengths, queries, *partials, *pieces)


def per_device(
    queries, keys, values, cache_keys, cache_values, doc_lengths, doc_owners, block_offsets
):
    count = lax.axis_size("ctx")
    even = lax.axis_index("ctx") % 2 == 0
    ring = lax.axis_size("req") == 2 and count <= RING_LIMIT
    slot = jnp.stack([cache_keys[0], cache_values[0]])
    own = jnp.stack([keys[0], values[0]])

    if ring:
        order = list(range(0, count, 2)) + list(range(1, count, 2))[::-1]
        onward = [(order[i], order[(i + 1) % count]) for i in range(count)]
        both = onward + [(count + target, count + source) for source, target in onward]
        pieces = [slot] + [None] * (count - 1)
        for step in range(1, count // 2 + 1):
            with jax.named_scope(f"ring{step}"):
                pieces[step] = lax.ppermute(pieces[step - 1], ("req", "ctx"), both)
            if 2 * step < count:
                with jax.named_scope(f"exchange{step}"):
                    pieces[count - step] = shifted(pieces[step], "req", 1)
    else:
        pieces = [broadcast(slot, "ctx", doc_owners[number]) for number in range(DOCS)]

    with jax.named_scope("two"):
        two = shifted(own, "ctx", 2)
    with jax.named_scope("swapped"):
        swapped = lax.ppermute(two, "ctx", [(i, i ^ 1) for i in range(count)])
    with jax.named_scope("passed"):
        passed = shifted(jnp.where(even, own, two), "ctx", 1)

    partials = attend_window(queries[0], (own, two, swapped, passed), block_offsets)
    attended = attend_documents(queries[0], partials, pieces, ring, doc_owners, doc_lengths)
    return attended[None]


def solution(mesh):
    return jax.shard_map(
        per_device,
        mesh=mesh,
        in_specs=(
            P(("groups", "req"), "ctx", None),
            P(("groups", "req"), "ctx", None),
            P(("groups", "req"), "ctx", None),
            P(("groups", "ctx"), None, None),
            P(("groups", "ctx"), None, None),
            P("groups"),
            P("groups"),
            P("groups"),
        ),
        out_specs=P(("groups", "req"), "ctx", None),
        check_vma=False,
    )
```

```python
import functools
import math

import jax
import jax.numpy as jnp
from jax import lax
from jax.experimental import pallas as pl
from jax.experimental.pallas import tpu as pltpu
from jax.sharding import PartitionSpec as P


HD = 128
DOCS = 2
TILE = {"near": 2, "middle": 2, "far": 4}
RING_LIMIT = 16

NEGATIVE = -1e30
SCALE = math.log2(math.e) / math.sqrt(HD)


def broadcast(block, axis, source):
    block = jnp.where(lax.axis_index(axis) == source, block, jnp.zeros_like(block))
    return lax.psum(block, axis)


def shifted(value, axis, steps):
    count = lax.axis_size(axis)
    pairs = [(source, (source + steps) % count) for source in range(count)]
    return lax.ppermute(value, axis, pairs)


def bias_rows(keys, start, height, live):
    lane = lax.broadcasted_iota(jnp.int32, (height, HD), 1)
    row = lax.broadcasted_iota(jnp.int32, (height, HD), 0)
    dead = (row >= live) & (lane == 0)
    keys[start : start + height, HD:] = jnp.where(dead, NEGATIVE, 0.0).astype(jnp.bfloat16)


def ring_place(index, count):
    return jnp.where(index % 2 == 0, index // 2, count - 1 - index // 2)


def slot_gap(owner):
    count = lax.axis_size("ctx")
    gap = ring_place(lax.axis_index("ctx"), count) - ring_place(owner, count)
    gap = jnp.where(lax.axis_index("req") == 0, gap, -gap)
    return jnp.where(gap < 0, gap + count, gap)


def attention_body(group, tile, hops, labels, which, carried, final, scalars, *refs):
    requests = scalars.shape[0] - 2 * DOCS
    offsets = scalars
    owners = [scalars[requests + number] for number in range(DOCS)]
    refs = list(refs)
    take = lambda number: [refs.pop(0) for _ in range(number)]
    (q_ref,) = take(1)
    blocks = take(len(hops))
    slots = [take(2) for _ in labels] if which else []
    before = take(3) if carried else None
    (out_ref,) = take(1)
    sum_ref, top_ref = (None, None) if final else take(2)
    keys, values = refs
    tokens = q_ref.shape[0]
    height = slots[0][0].shape[0] if which else 0
    base = len(hops) * tokens
    ring = labels is not None and len(labels) > 0 and labels[0] is not None
    head_index = pl.program_id(0)
    documents = []
    if which and ring:
        count = lax.axis_size("ctx")
        gaps = [slot_gap(owners[number]) for number in range(DOCS)]
        late = (gaps[0] == count // 2) if count % 2 == 0 else False
        early = jnp.where(late, 1, 0)
        for place in which:
            number = early if place == 0 else 1 - early
            gap = jnp.where(number == 0, gaps[0], gaps[1])
            documents.append((number, gap))
    elif which:
        documents = [(place, place) for place in which]

    @pl.when(head_index == 0)
    def _():
        values[:, HD:] = jnp.ones((values.shape[0], HD), jnp.bfloat16)
        count = lax.axis_size("ctx")
        placed = lax.axis_index("ctx") - offsets[lax.axis_index("req")] + count
        placed = lax.rem(placed, count)
        for number, hop in enumerate(hops):
            bias_rows(keys, number * tokens, tokens, jnp.where(placed >= hop, tokens, 0))
        for place, (number, _) in enumerate(documents):
            bias_rows(keys, base + place * height, height, scalars[requests + DOCS + number])

    columns = pl.ds(pl.multiple_of(head_index * HD, HD), HD)
    for number, ref in enumerate(blocks):
        keys[number * tokens : (number + 1) * tokens, :HD] = ref[0, :, columns]
        values[number * tokens : (number + 1) * tokens, :HD] = ref[1, :, columns]
    for place, (_, gap) in enumerate(documents):
        rows = slice(base + place * height, base + (place + 1) * height)
        for index, (key_ref, value_ref) in enumerate(slots):

            @pl.when(gap == (labels[index] if ring else index))
            def _():
                keys[rows, :HD] = key_ref[:, columns]
                values[rows, :HD] = value_ref[:, columns]

    lane = lax.broadcasted_iota(jnp.int32, (tile * tokens, HD), 1)
    first = jnp.where(lane == 0, 1.0, 0.0).astype(jnp.bfloat16)
    if 0 in hops:
        query = lax.broadcasted_iota(jnp.int32, (tokens, tokens), 0)
        key = lax.broadcasted_iota(jnp.int32, (tokens, tokens), 1)
        causal = jnp.concatenate([key <= query] * tile, axis=0)

    def scored(head):
        heads = []
        for i in range(head, head + tile):
            begin = pl.multiple_of((head_index * group + i) * HD, HD)
            heads.append(q_ref[:, pl.ds(begin, HD)])
        block = jnp.concatenate([jnp.concatenate(heads, axis=0), first], axis=1)
        scores = lax.dot_general(
            block, keys[...], (((1,), (1,)), ((), ())), preferred_element_type=jnp.float32
        )
        if 0 in hops:
            masked = jnp.where(causal, scores[:, :tokens], NEGATIVE)
            scores = jnp.concatenate([masked, scores[:, tokens:]], axis=1)
        return scores

    def weighed(head, scores):
        highest = jnp.max(scores, axis=1, keepdims=True) * SCALE
        highest = jnp.broadcast_to(highest, (tile * tokens, HD))
        if carried:
            highest = jnp.maximum(highest, before[2][head_index, head * tokens : (head + tile) * tokens])
        repeated = jnp.concatenate([highest] * (scores.shape[1] // HD), axis=1)
        weights = jnp.exp2(scores * SCALE - repeated).astype(jnp.bfloat16)
        return highest, jnp.dot(weights, values[...], preferred_element_type=jnp.float32)

    def finish(head, highest, summed):
        rows = slice(head * tokens, (head + tile) * tokens)
        total, denominator = summed[:, :HD], summed[:, HD:]
        if carried:
            share = jnp.exp2(before[2][head_index, rows] - highest)
            total = total + before[0][head_index, rows] * share
            denominator = denominator + before[1][head_index, rows] * share
        if final:
            result = total / denominator
            for i in range(tile):
                columns_of = slice((head + i) * HD, (head + i + 1) * HD)
                out_ref[:, columns_of] = result[i * tokens : (i + 1) * tokens].astype(jnp.bfloat16)
        else:
            out_ref[head_index, rows] = total
            sum_ref[head_index, rows] = denominator
            top_ref[head_index, rows] = highest

    starts = list(range(0, group, tile))
    scores = scored(starts[0])
    pending = None
    for number, head in enumerate(starts):
        following = scored(starts[number + 1]) if number + 1 < len(starts) else None
        result = weighed(head, scores)
        if pending is not None:
            finish(*pending)
        pending = (head, *result)
        scores = following
    finish(*pending)


def attend(name, scalars, queries, blocks, slots, which, before, final):
    tokens, width = queries.shape
    kv_width = (blocks[0][1] if blocks else slots[0][1]).shape[-1]
    kv_heads = kv_width // HD
    group = width // kv_width
    rows = group * tokens
    heads = pl.BlockSpec((tokens, group * HD), lambda g, *s: (0, g))
    whole = pl.BlockSpec(memory_space=pltpu.VMEM)
    total = len(blocks) * tokens + (len(which) * slots[0][1].shape[0] if which else 0)
    operands = [queries] + [block for _, block in blocks]
    for _, key_rows, value_rows in slots:
        operands += [key_rows, value_rows]
    if before is not None:
        operands += before
    partials = jax.ShapeDtypeStruct((kv_heads, rows, HD), jnp.float32)
    return pl.pallas_call(
        functools.partial(
            attention_body,
            group,
            math.gcd(group, TILE[name]),
            tuple(hop for hop, _ in blocks),
            tuple(label for label, _, _ in slots),
            which,
            before is not None,
            final,
        ),
        out_shape=jax.ShapeDtypeStruct((tokens, width), jnp.bfloat16) if final else [partials] * 3,
        grid_spec=pltpu.PrefetchScalarGridSpec(
            num_scalar_prefetch=1,
            grid=(kv_heads,),
            in_specs=[whole] * len(operands),
            out_specs=heads if final else [whole] * 3,
            scratch_shapes=[pltpu.VMEM((total, 2 * HD), jnp.bfloat16)] * 2,
        ),
        compiler_params=pltpu.CompilerParams(vmem_limit_bytes=32 << 20),
        cost_estimate=pl.CostEstimate(
            flops=4 * kv_heads * rows * total * HD,
            bytes_accessed=8 * kv_heads * rows * HD,
            transcendentals=kv_heads * rows * total,
        ),
    )(scalars, *operands)


def per_device(
    queries, keys, values, cache_keys, cache_values, doc_lengths, doc_owners, block_offsets
):
    count = lax.axis_size("ctx")
    even = lax.axis_index("ctx") % 2 == 0
    ring = lax.axis_size("req") == 2 and count <= RING_LIMIT
    own = jnp.stack([keys[0], values[0]])
    slot = (cache_keys[0], cache_values[0])

    if ring:
        order = list(range(0, count, 2)) + list(range(1, count, 2))[::-1]
        onward = [(order[i], order[(i + 1) % count]) for i in range(count)]
        both = onward + [(count + target, count + source) for source, target in onward]
        pieces = [slot] + [[None, None] for _ in range(count - 1)]
        for step in range(1, count // 2 + 1):
            for part in range(2):
                pieces[step][part] = lax.ppermute(pieces[step - 1][part], ("req", "ctx"), both)
                if 2 * step < count:
                    pieces[count - step][part] = shifted(pieces[step][part], "req", 1)
    else:
        pieces = [
            [broadcast(part, "ctx", doc_owners[number]) for part in slot] for number in range(DOCS)
        ]

    two = shifted(own, "ctx", 2)
    one = lax.ppermute(jnp.where(even, own, two), "ctx", [(i, i ^ 1) for i in range(count)])
    three = shifted(one, "ctx", 2)

    scalars = jnp.concatenate([block_offsets, doc_owners, doc_lengths])
    labels = range(count) if ring else [None] * DOCS
    slots = [(label, *piece) for label, piece in zip(labels, pieces)]
    soon = [s for s in slots if not (ring and 2 * s[0] == count)]
    window = [(0, own), (1, one), (2, two)]
    state = attend("near", scalars, queries[0], window, [], (), None, False)
    state = attend("middle", scalars, queries[0], [(3, three)], soon, (0,), state, False)
    return attend("far", scalars, queries[0], [], slots, (1,), state, True)[None]


def solution(mesh):
    return jax.shard_map(
        per_device,
        mesh=mesh,
        in_specs=(
            P(("groups", "req"), "ctx", None),
            P(("groups", "req"), "ctx", None),
            P(("groups", "req"), "ctx", None),
            P(("groups", "ctx"), None, None),
            P(("groups", "ctx"), None, None),
            P("groups"),
            P("groups"),
            P("groups"),
        ),
        out_specs=P(("groups", "req"), "ctx", None),
        check_vma=False,
    )
```

```python
import functools
import math

import jax
import jax.numpy as jnp
from jax import lax
from jax.experimental import pallas as pl
from jax.experimental.pallas import tpu as pltpu
from jax.sharding import PartitionSpec as P


HD = 128
DOCS = 2
HEADROOM = 40.0
TILE = {"near": 2, "middle": 2, "far": 4}
RING_LIMIT = 16

NEGATIVE = -1e30
SCALE = math.log2(math.e) / math.sqrt(HD)


def broadcast(block, axis, source):
    block = jnp.where(lax.axis_index(axis) == source, block, jnp.zeros_like(block))
    return lax.psum(block, axis)


def shifted(value, axis, steps):
    count = lax.axis_size(axis)
    pairs = [(source, (source + steps) % count) for source in range(count)]
    return lax.ppermute(value, axis, pairs)


def bias_rows(keys, start, height, live):
    lane = lax.broadcasted_iota(jnp.int32, (height, HD), 1)
    row = lax.broadcasted_iota(jnp.int32, (height, HD), 0)
    dead = (row >= live) & (lane == 0)
    bias = jnp.where(dead, NEGATIVE, 0.0).astype(jnp.bfloat16)
    for g in range(keys.shape[0]):
        keys[g, start : start + height, HD:] = bias


def ring_place(index, count):
    return jnp.where(index % 2 == 0, index // 2, count - 1 - index // 2)


def slot_gap(owner):
    count = lax.axis_size("ctx")
    gap = ring_place(lax.axis_index("ctx"), count) - ring_place(owner, count)
    gap = jnp.where(lax.axis_index("req") == 0, gap, -gap)
    return jnp.where(gap < 0, gap + count, gap)


def attention_body(kv_heads, group, tile, hops, paired, labels, which, carried, final, scalars, *refs):
    requests = scalars.shape[0] - 2 * DOCS
    offsets = scalars
    owners = [scalars[requests + number] for number in range(DOCS)]
    refs = list(refs)
    take = lambda number: [refs.pop(0) for _ in range(number)]
    (q_ref,) = take(1)
    blocks = [take(1 if stacked else 2) for stacked in paired]
    slots = [take(2) for _ in labels] if which else []
    before = take(3) if carried else None
    (out_ref,) = take(1)
    sum_ref, top_ref = (None, None) if final else take(2)
    keys, values = take(2)
    staged, sems = take(2) if final else (None, None)
    tokens = q_ref.shape[0]
    height = slots[0][0].shape[0] if which else 0
    base = len(hops) * tokens
    ring = len(labels) > 0 and labels[0] is not None
    count = lax.axis_size("ctx")
    documents = []
    if which and ring:
        gaps = [slot_gap(owners[number]) for number in range(DOCS)]
        late = (gaps[0] == count // 2) if count % 2 == 0 else False
        early = jnp.where(late, 1, 0)
        for place in which:
            number = early if place == 0 else 1 - early
            gap = jnp.where(number == 0, gaps[0], gaps[1])
            documents.append((number, gap))
    elif which:
        documents = [(place, place) for place in which]

    placed = lax.axis_index("ctx") - offsets[lax.axis_index("req")] + count
    placed = lax.rem(placed, count)
    ones = jnp.ones((values.shape[1], HD), jnp.bfloat16)
    for number, hop in enumerate(hops):
        bias_rows(keys, number * tokens, tokens, jnp.where(placed >= hop, tokens, 0))
    for place, (number, _) in enumerate(documents):
        bias_rows(keys, base + place * height, height, scalars[requests + DOCS + number])
    for g in range(kv_heads):
        values[g, :, HD:] = ones
        for number, ref in enumerate(blocks):
            rows = slice(number * tokens, (number + 1) * tokens)
            both = [part.at[i] for part in ref for i in range(2)] if len(ref) == 1 else ref
            keys[g, rows, :HD] = both[0][:, g * HD : (g + 1) * HD]
            values[g, rows, :HD] = both[1][:, g * HD : (g + 1) * HD]
    for place, (_, gap) in enumerate(documents):
        rows = slice(base + place * height, base + (place + 1) * height)
        for index, (key_ref, value_ref) in enumerate(slots):

            @pl.when(gap == (labels[index] if ring else index))
            def _():
                for g in range(kv_heads):
                    keys[g, rows, :HD] = key_ref[:, g * HD : (g + 1) * HD]
                    values[g, rows, :HD] = value_ref[:, g * HD : (g + 1) * HD]

    lane = lax.broadcasted_iota(jnp.int32, (tile * tokens, HD), 1)
    first = jnp.where(lane == 0, 1.0, 0.0).astype(jnp.bfloat16)
    if 0 in hops:
        query = lax.broadcasted_iota(jnp.int32, (tokens, tokens), 0)
        key = lax.broadcasted_iota(jnp.int32, (tokens, tokens), 1)
        causal = jnp.concatenate([key <= query] * tile, axis=0)

    def scored(g, head):
        begin = g * group + head
        heads = [q_ref[:, i * HD : (i + 1) * HD] for i in range(begin, begin + tile)]
        block = jnp.concatenate([jnp.concatenate(heads, axis=0), first], axis=1)
        scores = lax.dot_general(
            block, keys[g], (((1,), (1,)), ((), ())), preferred_element_type=jnp.float32
        )
        if 0 in hops:
            masked = jnp.where(causal, scores[:, :tokens], NEGATIVE)
            scores = jnp.concatenate([masked, scores[:, tokens:]], axis=1)
        return scores

    def weighed(g, head, scores, fast):
        rows = slice(head * tokens, (head + tile) * tokens)
        if fast:
            highest = before[2][g, rows]
        else:
            highest = jnp.max(scores, axis=1, keepdims=True) * SCALE
            highest = jnp.broadcast_to(highest, (tile * tokens, HD))
            if carried:
                highest = jnp.maximum(highest, before[2][g, rows])
        repeated = jnp.concatenate([highest] * (scores.shape[1] // HD), axis=1)
        exponents = scores * SCALE - repeated
        if fast:
            parts = [exponents[:, i : i + HD] for i in range(0, exponents.shape[1], HD)]
            peak = functools.reduce(jnp.maximum, parts)
            peaks.append(jnp.max(peak.reshape(-1, 8, HD), axis=0))
        weights = jnp.exp2(exponents).astype(jnp.bfloat16)
        return highest, jnp.dot(weights, values[g], preferred_element_type=jnp.float32)

    def finish(g, head, highest, summed, fast):
        rows = slice(head * tokens, (head + tile) * tokens)
        total, denominator = summed[:, :HD], summed[:, HD:]
        if fast:
            total = total + before[0][g, rows]
            denominator = denominator + before[1][g, rows]
        elif carried:
            share = jnp.exp2(before[2][g, rows] - highest)
            total = total + before[0][g, rows] * share
            denominator = denominator + before[1][g, rows] * share
        if final:
            result = (total / denominator).astype(jnp.bfloat16)
            for i in range(tile):
                begin = (g * group + head + i) * HD
                staged[:, begin : begin + HD] = result[i * tokens : (i + 1) * tokens]
            if head + tile == group:
                store(g).start()
        else:
            out_ref[g, rows] = total
            sum_ref[g, rows] = denominator
            top_ref[g, rows] = highest

    def store(g):
        columns = pl.ds(g * group * HD, group * HD)
        return pltpu.make_async_copy(staged.at[:, columns], out_ref.at[:, columns], sems.at[g])

    def run(fast):
        starts = [(g, head) for g in range(kv_heads) for head in range(0, group, tile)]
        scores = scored(*starts[0])
        pending = None
        for number, where in enumerate(starts):
            following = scored(*starts[number + 1]) if number + 1 < len(starts) else None
            result = weighed(*where, scores, fast)
            if pending is not None:
                finish(*pending, fast)
            pending = (*where, *result)
            scores = following
        finish(*pending, fast)
        if final:
            for g in range(kv_heads):
                store(g).wait()

    peaks = []
    run(carried)
    if carried:

        @pl.when(jnp.max(functools.reduce(jnp.maximum, peaks)) > HEADROOM)
        def _():
            run(False)


def fetch_body(queries, keys, values, to_queries, to_block, sems):
    pairs = [(queries, to_queries), (keys, to_block.at[0]), (values, to_block.at[1])]
    copies = [pltpu.make_async_copy(*pair, sems.at[i]) for i, pair in enumerate(pairs)]
    for copy in copies:
        copy.start()
    for copy in copies:
        copy.wait()


def fetch(queries, keys, values):
    return pl.pallas_call(
        fetch_body,
        out_shape=[
            jax.ShapeDtypeStruct(queries.shape, queries.dtype),
            jax.ShapeDtypeStruct((2,) + keys.shape, keys.dtype),
        ],
        in_specs=[pl.BlockSpec(memory_space=pl.ANY)] * 3,
        out_specs=[pl.BlockSpec(memory_space=pltpu.VMEM)] * 2,
        scratch_shapes=[pltpu.SemaphoreType.DMA((3,))],
        compiler_params=pltpu.CompilerParams(vmem_limit_bytes=4 << 20),
        name="fetch",
    )(queries, keys, values)


def attend(name, scalars, queries, blocks, slots, which, before, final):
    tokens, width = queries.shape
    kv_width = (blocks[0][1] if blocks else slots[0][1]).shape[-1]
    kv_heads = kv_width // HD
    group = width // kv_width
    rows = group * tokens
    whole = pl.BlockSpec(memory_space=pltpu.VMEM)
    total = len(blocks) * tokens + (len(which) * slots[0][1].shape[0] if which else 0)
    operands = [queries, *sum((list(block[1:]) for block in blocks), [])]
    for _, key_rows, value_rows in slots:
        operands += [key_rows, value_rows]
    if before is not None:
        operands += before
    stage = [pltpu.VMEM((tokens, width), jnp.bfloat16), pltpu.SemaphoreType.DMA((kv_heads,))]
    stage = stage if final else []
    partials = jax.ShapeDtypeStruct((kv_heads, rows, HD), jnp.float32)
    return pl.pallas_call(
        functools.partial(
            attention_body,
            kv_heads,
            group,
            math.gcd(group, TILE[name]),
            tuple(block[0] for block in blocks),
            tuple(len(block) == 2 for block in blocks),
            tuple(label for label, _, _ in slots),
            which,
            before is not None,
            final,
        ),
        out_shape=jax.ShapeDtypeStruct((tokens, width), jnp.bfloat16) if final else [partials] * 3,
        grid_spec=pltpu.PrefetchScalarGridSpec(
            num_scalar_prefetch=1,
            in_specs=[whole] * len(operands),
            out_specs=pl.BlockSpec(memory_space=pl.ANY) if final else [whole] * 3,
            scratch_shapes=[pltpu.VMEM((kv_heads, total, 2 * HD), jnp.bfloat16)] * 2 + stage,
        ),
        compiler_params=pltpu.CompilerParams(vmem_limit_bytes=24 << 20),
        cost_estimate=pl.CostEstimate(
            flops=4 * kv_heads * rows * total * HD,
            bytes_accessed=8 * kv_heads * rows * HD,
            transcendentals=kv_heads * rows * total,
        ),
    )(scalars, *operands)


def per_device(
    queries, keys, values, cache_keys, cache_values, doc_lengths, doc_owners, block_offsets
):
    count = lax.axis_size("ctx")
    even = lax.axis_index("ctx") % 2 == 0
    ring = lax.axis_size("req") == 2 and count <= RING_LIMIT
    own = (keys[0], values[0])
    slot = (cache_keys[0], cache_values[0])

    if ring:
        order = list(range(0, count, 2)) + list(range(1, count, 2))[::-1]
        onward = [(order[i], order[(i + 1) % count]) for i in range(count)]
        both = onward + [(count + target, count + source) for source, target in onward]
        pieces = [slot] + [[None, None] for _ in range(count - 1)]
        for step in range(1, count // 2 + 1):
            for part in range(2):
                pieces[step][part] = lax.ppermute(pieces[step - 1][part], ("req", "ctx"), both)
                if 2 * step < count:
                    pieces[count - step][part] = shifted(pieces[step][part], "req", 1)
    else:
        pieces = [
            [broadcast(part, "ctx", doc_owners[number]) for part in slot] for number in range(DOCS)
        ]

    two = [None, None]
    for part in range(2):
        two[part] = shifted(own[part], "ctx", 2)
    scalars = jnp.concatenate([block_offsets, doc_owners, doc_lengths])
    taken = jnp.stack([jnp.where(even, own[part], two[part]) for part in range(2)])
    taken, scalars = lax.optimization_barrier((taken, scalars))
    one = lax.ppermute(taken, "ctx", [(i, i ^ 1) for i in range(count)])
    three = shifted(one, "ctx", 2)

    labels = range(count) if ring else [None] * DOCS
    slots = [(label, *piece) for label, piece in zip(labels, pieces)]
    soon = [s for s in slots if not (ring and 2 * s[0] == count)]
    held, block = fetch(queries[0], *own)
    window = [(0, block), (1, one), (2, *two)]
    state = attend("near", scalars, held, window, [], (), None, False)
    state = attend("middle", scalars, held, [(3, three)], soon, (0,), state, False)
    return attend("far", scalars, held, [], slots, (1,), state, True)[None]


def solution(mesh):
    return jax.shard_map(
        per_device,
        mesh=mesh,
        in_specs=(
            P(("groups", "req"), "ctx", None),
            P(("groups", "req"), "ctx", None),
            P(("groups", "req"), "ctx", None),
            P(("groups", "ctx"), None, None),
            P(("groups", "ctx"), None, None),
            P("groups"),
            P("groups"),
            P("groups"),
        ),
        out_specs=P(("groups", "req"), "ctx", None),
        check_vma=False,
    )
```

```python
import functools
import math

import jax
import jax.numpy as jnp
from jax import lax
from jax.experimental import pallas as pl
from jax.experimental.pallas import tpu as pltpu
from jax.sharding import PartitionSpec as P


HD = 128
DOCS = 2
HEADROOM = 40.0
TILE = {"near": 2, "middle": 2, "far": 4}
RING_LIMIT = 16

NEGATIVE = -1e30
SCALE = math.log2(math.e) / math.sqrt(HD)


def broadcast(block, axis, source):
    block = jnp.where(lax.axis_index(axis) == source, block, jnp.zeros_like(block))
    return lax.psum(block, axis)


def shifted(value, axis, steps):
    count = lax.axis_size(axis)
    pairs = [(source, (source + steps) % count) for source in range(count)]
    return lax.ppermute(value, axis, pairs)


def bias_rows(keys, start, height, live):
    lane = lax.broadcasted_iota(jnp.int32, (height, HD), 1)
    row = lax.broadcasted_iota(jnp.int32, (height, HD), 0)
    dead = (row >= live) & (lane == 0)
    bias = jnp.where(dead, NEGATIVE, 0.0).astype(jnp.bfloat16)
    for g in range(keys.shape[0]):
        keys[g, start : start + height, HD:] = bias


def ring_place(index, count):
    return jnp.where(index % 2 == 0, index // 2, count - 1 - index // 2)


def slot_gap(owner):
    count = lax.axis_size("ctx")
    gap = ring_place(lax.axis_index("ctx"), count) - ring_place(owner, count)
    gap = jnp.where(lax.axis_index("req") == 0, gap, -gap)
    return jnp.where(gap < 0, gap + count, gap)


def attention_body(kv_heads, group, tile, hops, paired, labels, which, carried, final, scalars, *refs):
    requests = scalars.shape[0] - 2 * DOCS
    offsets = scalars
    owners = [scalars[requests + number] for number in range(DOCS)]
    refs = list(refs)
    take = lambda number: [refs.pop(0) for _ in range(number)]
    (q_ref,) = take(1)
    blocks = [take(1 if stacked else 2) for stacked in paired]
    slots = [take(2) for _ in labels] if which else []
    before = take(3) if carried else None
    (out_ref,) = take(1)
    sum_ref, top_ref = (None, None) if final else take(2)
    (both,) = take(1)
    keys, values = both.at[0], both.at[1]
    staged, sems = take(2) if final else (None, None)
    tokens = q_ref.shape[0]
    height = slots[0][0].shape[0] if which else 0
    base = len(hops) * tokens
    ring = len(labels) > 0 and labels[0] is not None
    count = lax.axis_size("ctx")
    documents = []
    if which and ring:
        gaps = [slot_gap(owners[number]) for number in range(DOCS)]
        late = (gaps[0] == count // 2) if count % 2 == 0 else False
        early = jnp.where(late, 1, 0)
        for place in which:
            number = early if place == 0 else 1 - early
            gap = jnp.where(number == 0, gaps[0], gaps[1])
            documents.append((number, gap))
    elif which:
        documents = [(place, place) for place in which]

    placed = lax.axis_index("ctx") - offsets[lax.axis_index("req")] + count
    placed = lax.rem(placed, count)
    ones = jnp.ones((values.shape[1], HD), jnp.bfloat16)
    for number, hop in enumerate(hops):
        bias_rows(keys, number * tokens, tokens, jnp.where(placed >= hop, tokens, 0))
    for place, (number, _) in enumerate(documents):
        bias_rows(keys, base + place * height, height, scalars[requests + DOCS + number])
    for g in range(kv_heads):
        values[g, :, HD:] = ones
        for number, ref in enumerate(blocks):
            rows = slice(number * tokens, (number + 1) * tokens)
            pair = [part.at[i] for part in ref for i in range(2)] if len(ref) == 1 else ref
            for kind in range(2):
                both[kind, g, rows, :HD] = pair[kind][:, g * HD : (g + 1) * HD]
    for place, (_, gap) in enumerate(documents):
        rows = slice(base + place * height, base + (place + 1) * height)
        for index, (first_ref, second_ref) in enumerate(slots):

            @pl.when(gap == (labels[index] if ring else index))
            def _():
                kind = 0
                if ring:
                    core = lax.axis_index("req")
                    kind = 1 - core if 2 * labels[index] > count else core
                for g in range(kv_heads):
                    columns = slice(g * HD, (g + 1) * HD)
                    both[kind, g, rows, :HD] = first_ref[:, columns]
                    both[1 - kind, g, rows, :HD] = second_ref[:, columns]

    lane = lax.broadcasted_iota(jnp.int32, (tile * tokens, HD), 1)
    first = jnp.where(lane == 0, 1.0, 0.0).astype(jnp.bfloat16)
    if 0 in hops:
        query = lax.broadcasted_iota(jnp.int32, (tokens, tokens), 0)
        key = lax.broadcasted_iota(jnp.int32, (tokens, tokens), 1)
        causal = jnp.concatenate([key <= query] * tile, axis=0)

    def scored(g, head):
        begin = g * group + head
        heads = [q_ref[:, i * HD : (i + 1) * HD] for i in range(begin, begin + tile)]
        block = jnp.concatenate([jnp.concatenate(heads, axis=0), first], axis=1)
        scores = lax.dot_general(
            block, keys[g], (((1,), (1,)), ((), ())), preferred_element_type=jnp.float32
        )
        if 0 in hops:
            masked = jnp.where(causal, scores[:, :tokens], NEGATIVE)
            scores = jnp.concatenate([masked, scores[:, tokens:]], axis=1)
        return scores

    def weighed(g, head, scores, fast):
        rows = slice(head * tokens, (head + tile) * tokens)
        if fast:
            highest = before[2][g, rows]
        else:
            highest = jnp.max(scores, axis=1, keepdims=True) * SCALE
            highest = jnp.broadcast_to(highest, (tile * tokens, HD))
            if carried:
                highest = jnp.maximum(highest, before[2][g, rows])
        repeated = jnp.concatenate([highest] * (scores.shape[1] // HD), axis=1)
        exponents = scores * SCALE - repeated
        if fast:
            parts = [exponents[:, i : i + HD] for i in range(0, exponents.shape[1], HD)]
            peak = functools.reduce(jnp.maximum, parts)
            peaks.append(jnp.max(peak.reshape(-1, 8, HD), axis=0))
        weights = jnp.exp2(exponents).astype(jnp.bfloat16)
        return highest, jnp.dot(weights, values[g], preferred_element_type=jnp.float32)

    def finish(g, head, highest, summed, fast):
        rows = slice(head * tokens, (head + tile) * tokens)
        total, denominator = summed[:, :HD], summed[:, HD:]
        if fast:
            total = total + before[0][g, rows]
            denominator = denominator + before[1][g, rows]
        elif carried:
            share = jnp.exp2(before[2][g, rows] - highest)
            total = total + before[0][g, rows] * share
            denominator = denominator + before[1][g, rows] * share
        if final:
            result = (total / denominator).astype(jnp.bfloat16)
            for i in range(tile):
                begin = (g * group + head + i) * HD
                staged[:, begin : begin + HD] = result[i * tokens : (i + 1) * tokens]
            if head + tile == group:
                store(g).start()
        else:
            out_ref[g, rows] = total
            sum_ref[g, rows] = denominator
            top_ref[g, rows] = highest

    def store(g):
        columns = pl.ds(g * group * HD, group * HD)
        return pltpu.make_async_copy(staged.at[:, columns], out_ref.at[:, columns], sems.at[g])

    def run(fast):
        starts = [(g, head) for g in range(kv_heads) for head in range(0, group, tile)]
        scores = scored(*starts[0])
        pending = None
        for number, where in enumerate(starts):
            following = scored(*starts[number + 1]) if number + 1 < len(starts) else None
            result = weighed(*where, scores, fast)
            if pending is not None:
                finish(*pending, fast)
            pending = (*where, *result)
            scores = following
        finish(*pending, fast)
        if final:
            for g in range(kv_heads):
                store(g).wait()

    peaks = []
    run(carried)
    if carried:

        @pl.when(jnp.max(functools.reduce(jnp.maximum, peaks)) > HEADROOM)
        def _():
            run(False)


def fetch_body(queries, keys, values, to_queries, to_block, sems):
    pairs = [(queries, to_queries), (keys, to_block.at[0]), (values, to_block.at[1])]
    copies = [pltpu.make_async_copy(*pair, sems.at[i]) for i, pair in enumerate(pairs)]
    for copy in copies:
        copy.start()
    for copy in copies:
        copy.wait()


def fetch(queries, keys, values):
    return pl.pallas_call(
        fetch_body,
        out_shape=[
            jax.ShapeDtypeStruct(queries.shape, queries.dtype),
            jax.ShapeDtypeStruct((2,) + keys.shape, keys.dtype),
        ],
        in_specs=[pl.BlockSpec(memory_space=pl.ANY)] * 3,
        out_specs=[pl.BlockSpec(memory_space=pltpu.VMEM)] * 2,
        scratch_shapes=[pltpu.SemaphoreType.DMA((3,))],
        compiler_params=pltpu.CompilerParams(vmem_limit_bytes=4 << 20),
        name="fetch",
    )(queries, keys, values)


def attend(name, scalars, queries, blocks, slots, which, before, final):
    tokens, width = queries.shape
    kv_width = (blocks[0][1] if blocks else slots[0][1]).shape[-1]
    kv_heads = kv_width // HD
    group = width // kv_width
    rows = group * tokens
    whole = pl.BlockSpec(memory_space=pltpu.VMEM)
    total = len(blocks) * tokens + (len(which) * slots[0][1].shape[0] if which else 0)
    operands = [queries, *sum((list(block[1:]) for block in blocks), [])]
    for _, key_rows, value_rows in slots:
        operands += [key_rows, value_rows]
    if before is not None:
        operands += before
    stage = [pltpu.VMEM((tokens, width), jnp.bfloat16), pltpu.SemaphoreType.DMA((kv_heads,))]
    stage = stage if final else []
    partials = jax.ShapeDtypeStruct((kv_heads, rows, HD), jnp.float32)
    return pl.pallas_call(
        functools.partial(
            attention_body,
            kv_heads,
            group,
            math.gcd(group, TILE[name]),
            tuple(block[0] for block in blocks),
            tuple(len(block) == 2 for block in blocks),
            tuple(label for label, _, _ in slots),
            which,
            before is not None,
            final,
        ),
        out_shape=jax.ShapeDtypeStruct((tokens, width), jnp.bfloat16) if final else [partials] * 3,
        grid_spec=pltpu.PrefetchScalarGridSpec(
            num_scalar_prefetch=1,
            in_specs=[whole] * len(operands),
            out_specs=pl.BlockSpec(memory_space=pl.ANY) if final else [whole] * 3,
            scratch_shapes=[pltpu.VMEM((2, kv_heads, total, 2 * HD), jnp.bfloat16)] + stage,
        ),
        compiler_params=pltpu.CompilerParams(vmem_limit_bytes=24 << 20),
        cost_estimate=pl.CostEstimate(
            flops=4 * kv_heads * rows * total * HD,
            bytes_accessed=8 * kv_heads * rows * HD,
            transcendentals=kv_heads * rows * total,
        ),
    )(scalars, *operands)


def per_device(
    queries, keys, values, cache_keys, cache_values, doc_lengths, doc_owners, block_offsets
):
    count = lax.axis_size("ctx")
    even = lax.axis_index("ctx") % 2 == 0
    ring = lax.axis_size("req") == 2 and count <= RING_LIMIT
    own = (keys[0], values[0])
    slot = (cache_keys[0], cache_values[0])

    if ring:
        order = list(range(0, count, 2)) + list(range(1, count, 2))[::-1]
        onward = [(order[i], order[(i + 1) % count]) for i in range(count)]
        both = onward + [(count + target, count + source) for source, target in onward]
        turned = lax.axis_index("req") == 1
        slot = (jnp.where(turned, slot[1], slot[0]), jnp.where(turned, slot[0], slot[1]))
        pieces = [slot] + [[None, None] for _ in range(count - 1)]
        for step in range(1, count // 2 + 1):
            last = 2 * step == count
            for part in range(1 if last else 2):
                pieces[step][part] = lax.ppermute(pieces[step - 1][part], ("req", "ctx"), both)
                brought = shifted(pieces[step][part], "req", 1)
                if last:
                    pieces[step][1] = brought
                else:
                    pieces[count - step][part] = brought
    else:
        pieces = [
            [broadcast(part, "ctx", doc_owners[number]) for part in slot] for number in range(DOCS)
        ]

    two = [None, None]
    for part in range(2):
        two[part] = shifted(own[part], "ctx", 2)
    scalars = jnp.concatenate([block_offsets, doc_owners, doc_lengths])
    taken = jnp.stack([jnp.where(even, own[part], two[part]) for part in range(2)])
    taken, scalars = lax.optimization_barrier((taken, scalars))
    one = lax.ppermute(taken, "ctx", [(i, i ^ 1) for i in range(count)])
    three = shifted(one, "ctx", 2)

    labels = range(count) if ring else [None] * DOCS
    slots = [(label, *piece) for label, piece in zip(labels, pieces)]
    soon = [s for s in slots if not (ring and 2 * s[0] == count)]
    held, block = fetch(queries[0], *own)
    state = attend("near", scalars, held, [(0, block), (2, *two)], [], (), None, False)
    state = attend("middle", scalars, held, [(1, one)], soon, (0,), state, False)
    return attend("far", scalars, held, [(3, three)], slots, (1,), state, True)[None]


def solution(mesh):
    return jax.shard_map(
        per_device,
        mesh=mesh,
        in_specs=(
            P(("groups", "req"), "ctx", None),
            P(("groups", "req"), "ctx", None),
            P(("groups", "req"), "ctx", None),
            P(("groups", "ctx"), None, None),
            P(("groups", "ctx"), None, None),
            P("groups"),
            P("groups"),
            P("groups"),
        ),
        out_specs=P(("groups", "req"), "ctx", None),
        check_vma=False,
    )
```
